32 devices in a mesh: depth: 4 (over z), row: 2 (over core), col: 4 (over y, x).
Axes of the slice: x: 2, y: 2, z: 4, core: 2. Of those that a mesh axis runs over, the one named last changes fastest.
Arguments:
- volume: bfloat16 [4, 18, 256, 8192], P('depth', None, 'row', 'col'), may hold values from -6 to 6
- order: int32 [4], replicated, may hold values from 0 to 3, each once
- empty: int32 [4, 2, 4], P('depth', 'row', 'col'), may hold values 0 or 1
- bump_center: float32 [4], replicated, may hold values from -1.5 to 1.5
- bump_width: float32 [4], replicated, may hold values from 0.3 to 1
- bump_height: float32 [4], replicated, may hold values from 0.5 to 4
- bump_color: float32 [3, 4], replicated, may hold values from 0.5 to 2
- light_dir: float32 [3], replicated, may hold values from -1 to 1
Outputs:
- image: float32 [2, 4, 128, 8192], P('row', None, 'depth', 'col')
The draws below stay inside these ranges and needn't reach their ends.
Inputs may be any that keep to these rules, and one draw needn't show every extreme that they name: `order`: a permutation of the depth indices.
All inputs are finite; a program needn't handle non-finite values. No bound on the sum of `empty` on one device may be relied on, other than what follows from the above.
Results may differ from the reference program's by a relative error of at most 0.0003.
Values may be sent and summed in bfloat16 or wider, within the bound.
No kernel may reach another device: no remote copies, remote signals or barrier semaphores. Data moves between devices by JAX's collectives and lax.ppermute only.
A program may use at most 128 MiB of HBM per device.

```python
import math
import jax
import jax.numpy as jnp
from jax import lax

ZB = 16
RT = 128
CT = 2048
NG = 4
BAND = 256
W = 8192
N_DEPTH = 4
N_ROW = 2
N_COL = 4


def place_ends(result, key, least, high):
    shape = result.shape
    spot = [jax.random.randint(jax.random.fold_in(key, axis), (), 0, shape[axis]) for axis in range(len(shape))]
    result = result.at[tuple(spot)].set(least)
    longest = shape.index(max(shape))
    spot[longest] = (spot[longest] + 1) % shape[longest]
    return result.at[tuple(spot)].set(high)


def steps_of(stream_key, dims, split, low, largest):
    gain, own = 1.0, jax.random.fold_in(stream_key, 6)
    for position, blocks in split:
        heights = jnp.exp(jax.random.uniform(jax.random.fold_in(own, position), (blocks,), jnp.float32, low / len(split), largest / len(split)))
        gain = gain * jnp.repeat(heights, dims[position] // blocks).reshape([-1 if axis == position else 1 for axis in range(len(dims))])
    return gain


def gaussian(own_key, dims, width, most, shards=(), kind=jnp.bfloat16):
    entries = jax.random.normal(own_key, dims, jnp.float32) * width
    if len(shards) > 0:
        entries = steps_of(own_key, dims, shards, -0.22, 0.18) * entries
    return jnp.clip(entries, min=-most, max=most).astype(kind)


def setup_inputs(seed: int = 0) -> dict:
    streams_of = jax.random.split(jax.random.key(seed), 9)
    return {
        "volume": gaussian(streams_of[0], (N_DEPTH, ZB + 2, BAND, W), 1.0, 6.0, ((0, 4), (2, 2), (3, 4))),
        "order": jax.random.permutation(streams_of[1], N_DEPTH).astype(jnp.int32),
        "empty": place_ends((jax.random.randint(streams_of[2], (N_DEPTH, N_ROW, N_COL), 0, 4) < 1).astype(jnp.int32), jax.random.fold_in(streams_of[2], 1), 0, 1),
        "bump_center": jnp.clip(jax.random.uniform(streams_of[3], (NG,), jnp.float32, -1.5, 1.5), -1.5, 1.5),
        "bump_width": jnp.clip(jnp.exp(jax.random.uniform(streams_of[4], (NG,), jnp.float32, math.log(0.3), math.log(1.0))), 0.3, 1.0),
        "bump_height": jnp.clip(jnp.exp(jax.random.uniform(streams_of[5], (NG,), jnp.float32, math.log(0.5), math.log(4.0))), 0.5, 4.0),
        "bump_color": jnp.clip(jax.random.uniform(streams_of[6], (3, NG), jnp.float32, 0.5, 2.0), 0.5, 2.0),
        "light_dir": jnp.clip(jax.random.uniform(streams_of[7], (3,), jnp.float32, -1.0, 1.0), -1.0, 1.0),
    }


slab_depth = 8
absorption = 0.08

def march_brick(padded, bump_center, bump_width, bump_height, bump_color, light_dir):
    depth_len = padded.shape[0] - 2
    row_count = padded.shape[1] - 2
    col_count = padded.shape[2] - 2
    per_sample = absorption / depth_len

    def advance(state_pair, slab_index):
        through, radiance = state_pair
        block_cells = lax.dynamic_slice_in_dim(padded, slab_index * slab_depth, slab_depth + 2, 0).astype(jnp.float32)
        samples = block_cells[1:-1, 1:-1, 1:-1]
        grad_z = 0.5 * (block_cells[2:, 1:-1, 1:-1] - block_cells[:-2, 1:-1, 1:-1])
        grad_y = 0.5 * (block_cells[1:-1, 2:, 1:-1] - block_cells[1:-1, :-2, 1:-1])
        grad_x = 0.5 * (block_cells[1:-1, 1:-1, 2:] - block_cells[1:-1, 1:-1, :-2])
        facing = jnp.abs(light_dir[0] * grad_z + light_dir[1] * grad_y + light_dir[2] * grad_x)
        shading = 0.3 + 0.7 * facing / jnp.sqrt(grad_z * grad_z + grad_y * grad_y + grad_x * grad_x + 1.0)
        density = jnp.zeros_like(samples)
        emission = [jnp.zeros_like(samples) for channel in range(3)]
        for bump_index in range(bump_center.shape[0]):
            offset = samples - bump_center[bump_index]
            bump_value = jnp.exp(-offset * offset / (2.0 * bump_width[bump_index] * bump_width[bump_index]))
            density = density + bump_height[bump_index] * bump_value
            emission = [emission[channel] + bump_color[channel, bump_index] * bump_value for channel in range(3)]
        passing = jnp.exp(-per_sample * density)
        inclusive = jnp.cumprod(passing, axis=0)
        transmit = jnp.concatenate([jnp.ones_like(passing[:1]), inclusive[:-1]], 0) * through
        weights = transmit * (1.0 - passing) * shading
        radiance = radiance + jnp.stack([lax.optimization_barrier(jnp.sum(weights * emission[channel], 0)) for channel in range(3)])
        return ((through * inclusive[-1], radiance), None)
    start_carry = (jnp.ones((row_count, col_count), jnp.float32), jnp.zeros((3, row_count, col_count), jnp.float32))
    (through, radiance), unused = lax.scan(advance, start_carry, jnp.arange(depth_len // slab_depth, dtype=jnp.int32))
    return jnp.concatenate([radiance, (1.0 - through)[None]], 0)

def composite(stacked, order):
    ranked = jnp.take(stacked, order, axis=0)

    def layer_over(state_pair, layer_image):
        through, summed = state_pair
        summed = summed + through[None] * layer_image
        return ((through * (1.0 - layer_image[3]), summed), None)
    start_carry = (jnp.ones(stacked.shape[2:], jnp.float32), jnp.zeros(stacked.shape[1:], jnp.float32))
    (through, summed), unused = lax.scan(layer_over, start_carry, ranked)
    return summed

def reference(volume, order, empty, bump_center, bump_width, bump_height, bump_color, light_dir):

    def one_brick(brick_index):
        padded = jnp.pad(volume[brick_index], ((0, 0), (1, 1), (1, 1)))
        layer_image = march_brick(padded, bump_center, bump_width, bump_height, bump_color, light_dir)
        empty_tile = jnp.repeat(jnp.repeat(empty[brick_index], RT, 0), CT, 1)
        return layer_image * (1 - empty_tile).astype(jnp.float32)[None]
    layers_all = lax.map(one_brick, jnp.arange(N_DEPTH, dtype=jnp.int32))
    summed = composite(layers_all, order)
    return summed.reshape(4, N_ROW, RT, W).transpose(1, 0, 2, 3)
```

```python
import math

import jax
import jax.numpy as jnp
from jax import lax
from jax.experimental import pallas as pl
from jax.experimental.pallas import tpu as pltpu
from jax.sharding import PartitionSpec as P

absorption = 0.08
LANES = 128
SUB = 8
LOG_MID = -12.5
LOG_HALF = 16.0
LOG_STEPS = 32767
LOW = -LOG_STEPS
VALUE_FLOOR = 2.0 ** (LOG_MID - LOG_HALF)


def encode(value):
    scale = LOG_STEPS / LOG_HALF
    log2v = jnp.log(jnp.maximum(value, VALUE_FLOOR)) * (scale / math.log(2.0))
    shifted = jnp.clip(log2v + (32768.5 - LOG_MID * scale), 1.0, 65535.5)
    return (shifted.astype(jnp.int32) - 32768).astype(jnp.int16)


def decode(code):
    wide = code.astype(jnp.int32).astype(jnp.float32)
    value = jnp.exp2(wide * (LOG_HALF / LOG_STEPS) + LOG_MID)
    return jnp.where(wide > LOW, value, 0.0)


def table(bump_center, bump_width, bump_height, bump_color, light_dir, depth_len):
    log2e = math.log2(math.e)
    strength = bump_height * (absorption / depth_len * log2e)
    square = -log2e / (2.0 * bump_width * bump_width)
    linear = -2.0 * square * bump_center
    constant = square * bump_center * bump_center + jnp.log2(strength)
    color = bump_color / strength[None]
    return jnp.concatenate([square, linear, constant, 0.7 * light_dir, color.reshape(-1)])


def march(volume, coef, info, row_halo, left_halo, right_halo, start, count, tiles, bumps, parts):
    planes, rows, cols = volume.shape
    depth_len = planes - 2
    width = tiles * LANES
    steps = count // tiles
    all_tiles = cols // LANES
    block = rows // parts
    has_left = left_halo is not None
    has_right = right_halo is not None

    def body(info_ref, coef_ref, vol, left, right, halo, *rest):
        rest = list(rest)
        lh = rest.pop(0) if has_left else None
        rh = rest.pop(0) if has_right else None
        outs, (cells, layer) = rest[:parts], rest[parts:]
        step = pl.program_id(0)
        me, row_at, row_last, is_empty = info_ref[0], info_ref[1], info_ref[2], info_ref[3]

        @pl.when(is_empty == 1)
        def _():
            outs[0][...] = jnp.zeros(outs[0].shape, jnp.float32)
            for k in range(1, parts):
                outs[k][...] = jnp.full(outs[k].shape, LOW, jnp.int16)

        @pl.when(is_empty != 1)
        def _():
            top_on = (row_at > 0).astype(jnp.float32)
            bottom_on = (row_at < row_last).astype(jnp.float32)
            for t in range(tiles):
                span = slice(LANES * t, LANES * (t + 1))
                cells[t + 1, :, SUB : SUB + rows, :] = vol[:, :, span].astype(jnp.float32)
                edge = halo[:, :, span].astype(jnp.float32)
                cells[t + 1, :, 0:SUB, :] = jnp.broadcast_to(edge[:, :1] * top_on, (planes, SUB, LANES))
                cells[t + 1, :, SUB + rows :, :] = jnp.broadcast_to(
                    edge[:, -1:] * bottom_on, (planes, SUB, LANES)
                )
            cells[0, :, SUB : SUB + rows, :] = left[...].astype(jnp.float32)
            cells[tiles + 1, :, SUB : SUB + rows, :] = right[...].astype(jnp.float32)
            if has_left:
                @pl.when(step == 0)
                def _():
                    cells[0, :, SUB : SUB + rows, :] = lh[...].astype(jnp.float32)
            if has_right:
                @pl.when(step == steps - 1)
                def _():
                    cells[tiles + 1, :, SUB : SUB + rows, :] = rh[...].astype(jnp.float32)

            square = [coef_ref[k] for k in range(bumps)]
            linear = [coef_ref[bumps + k] for k in range(bumps)]
            constant = [coef_ref[2 * bumps + k] for k in range(bumps)]
            light = [coef_ref[3 * bumps + k] for k in range(3)]
            color = [[coef_ref[3 * bumps + 3 + bumps * c + k] for k in range(bumps)] for c in range(3)]
            lane = lax.broadcasted_iota(jnp.int32, (SUB, LANES), 1)
            first = lane == 0
            last = lane == LANES - 1

            def strip(i, carry):
                base = pl.multiple_of(i * SUB, SUB)

                def load(t, s, shift=0):
                    return cells[t, s, pl.ds(base + (SUB + shift), SUB), :]

                zero = jnp.zeros((SUB, LANES), jnp.float32)
                before = [load(t + 1, 0) for t in range(tiles)]
                here = [load(t + 1, 1) for t in range(tiles)]
                depth = [zero] * tiles
                through = [zero + 1.0] * tiles
                total = [[zero] * bumps for t in range(tiles)]
                for s in range(1, depth_len + 1):
                    ahead = [load(t + 1, s + 1) for t in range(tiles)]
                    line = [load(0, s)] + here + [load(tiles + 1, s)]
                    up = [pltpu.roll(x, 1, 1) for x in line[:-1]]
                    down = [pltpu.roll(x, LANES - 1, 1) for x in line[1:]]
                    down.append(down[-1])
                    for t in range(tiles):
                        f = here[t]
                        grad_z = ahead[t] - before[t]
                        grad_y = load(t + 1, s, 1) - load(t + 1, s, -1)
                        right_of = jnp.where(last, pltpu.roll(line[t + 2], LANES - 1, 1), down[t])
                        left_of = jnp.where(first, up[t], pltpu.roll(line[t + 1], 1, 1))
                        grad_x = right_of - left_of
                        facing = jnp.abs(light[0] * grad_z + light[1] * grad_y + light[2] * grad_x)
                        norm = grad_z * grad_z + grad_y * grad_y + grad_x * grad_x + 4.0
                        shading = 0.3 + facing * lax.rsqrt(norm)
                        bump = [
                            jnp.exp2((square[k] * f + linear[k]) * f + constant[k]) for k in range(bumps)
                        ]
                        for k in range(bumps):
                            depth[t] = depth[t] - bump[k]
                        passed = jnp.exp2(depth[t])
                        weight = (through[t] - passed) * shading
                        through[t] = passed
                        total[t] = [total[t][k] + weight * bump[k] for k in range(bumps)]
                    before, here = here, ahead
                for t in range(tiles):
                    for c in range(3):
                        mixed = color[c][0] * total[t][0]
                        for k in range(1, bumps):
                            mixed = mixed + color[c][k] * total[t][k]
                        layer[c, pl.ds(base, SUB), LANES * t : LANES * (t + 1)] = mixed
                    layer[3, pl.ds(base, SUB), LANES * t : LANES * (t + 1)] = 1.0 - through[t]
                return carry

            lax.fori_loop(0, rows // SUB, strip, 0)
            for k in range(parts):
                at = pl.multiple_of(lax.rem(me + k, parts) * block, block)
                value = layer[:, pl.ds(at, block), :]
                outs[k][...] = value if k == 0 else encode(value)

    chunk = count * LANES
    tile0 = start // tiles
    in_specs = [
        pl.BlockSpec(memory_space=pltpu.SMEM),
        pl.BlockSpec(memory_space=pltpu.SMEM),
        pl.BlockSpec((planes, rows, width), lambda i: (0, 0, tile0 + i)),
        pl.BlockSpec((planes, rows, LANES), lambda i: (0, 0, jnp.maximum(start + i * tiles - 1, 0))),
        pl.BlockSpec(
            (planes, rows, LANES), lambda i: (0, 0, jnp.minimum(start + (i + 1) * tiles, all_tiles - 1))
        ),
        pl.BlockSpec((planes, row_halo.shape[1], width), lambda i: (0, 0, tile0 + i)),
    ]
    operands = [info, coef, volume, volume, volume, row_halo]
    for halo in (left_halo, right_halo):
        if halo is not None:
            in_specs.append(pl.BlockSpec((planes, rows, LANES), lambda i: (0, 0, 0)))
            operands.append(halo)
    return pl.pallas_call(
        body,
        grid=(steps,),
        out_shape=[
            jax.ShapeDtypeStruct((4, block, chunk), jnp.float32 if k == 0 else jnp.int16)
            for k in range(parts)
        ],
        in_specs=in_specs,
        out_specs=[pl.BlockSpec((4, block, width), lambda i: (0, 0, i)) for k in range(parts)],
        scratch_shapes=[
            pltpu.VMEM((tiles + 2, planes, rows + 2 * SUB, LANES), jnp.float32),
            pltpu.VMEM((4, rows, width), jnp.float32),
        ],
        compiler_params=pltpu.CompilerParams(vmem_limit_bytes=48 << 20),
        name="march",
    )(*operands)


def composite(own, coded, info, order, image, start, cols):
    parts = 1 + len(coded)
    channels, block, chunk = own.shape

    def body(info_ref, order_ref, own_ref, *rest):
        codes = rest[: parts - 1]
        out, layers = rest[-2], rest[-1]
        me = info_ref[0]
        layers[0] = own_ref[...]
        for k in range(1, parts):
            layers[k] = decode(codes[k - 1][...])
        through = jnp.ones((block, chunk), jnp.float32)
        summed = [jnp.zeros((block, chunk), jnp.float32)] * channels
        for place in range(parts):
            at = lax.rem(me - order_ref[place] + parts, parts)
            summed = [summed[c] + through * layers[at, c] for c in range(channels)]
            through = through * (1.0 - layers[at, 3])
        for c in range(channels):
            out[c] = summed[c]

    smem = pl.BlockSpec(memory_space=pltpu.SMEM)
    whole = pl.BlockSpec((channels, block, chunk), lambda i: (0, 0, 0))
    at_chunk = pl.BlockSpec((channels, block, chunk), lambda i: (0, 0, start * LANES // chunk))
    in_specs = [smem, smem, whole] + [whole] * (parts - 1)
    operands = [info, order, own, *coded]
    aliases = {}
    if image is not None:
        aliases = {len(operands): 0}
        operands.append(image)
        in_specs.append(pl.BlockSpec(memory_space=pl.ANY))
    return pl.pallas_call(
        body,
        grid=(1,),
        out_shape=jax.ShapeDtypeStruct((channels, block, cols), jnp.float32),
        in_specs=in_specs,
        out_specs=at_chunk,
        scratch_shapes=[pltpu.VMEM((parts, channels, block, chunk), jnp.float32)],
        input_output_aliases=aliases,
        compiler_params=pltpu.CompilerParams(vmem_limit_bytes=48 << 20),
        name="composite",
    )(*operands)


def per_device(volume, order, empty, bump_center, bump_width, bump_height, bump_color, light_dir):
    volume = volume[0]
    planes, rows, cols = volume.shape
    parts = lax.axis_size("depth")
    n_row = lax.axis_size("row")
    n_col = lax.axis_size("col")
    bumps = bump_center.shape[0]
    row_at = lax.axis_index("row")

    up = [(i, i + 1) for i in range(n_row - 1)]
    down = [(i + 1, i) for i in range(n_row - 1)]
    if n_row == 2:
        edge = lax.dynamic_slice(volume, (0, jnp.where(row_at == 0, rows - 1, 0), 0), (planes, 1, cols))
        row_halo = lax.ppermute(edge, "row", up + down)
    else:
        row_halo = jnp.concatenate(
            [
                lax.ppermute(volume[:, -1:], "row", up),
                lax.ppermute(volume[:, :1], "row", down),
            ],
            axis=1,
        )
    left_halo = lax.ppermute(volume[:, :, -LANES:], "col", [(i, i + 1) for i in range(n_col - 1)])
    right_halo = lax.ppermute(volume[:, :, :LANES], "col", [(i + 1, i) for i in range(n_col - 1)])

    coef = table(bump_center, bump_width, bump_height, bump_color, light_dir, planes - 2)
    me = lax.axis_index("depth")
    info = jnp.stack([me, row_at, jnp.int32(n_row - 1), empty[0, 0, 0]]).astype(jnp.int32)

    all_tiles = cols // LANES
    chunks = 4
    count = all_tiles // chunks
    image = None
    waiting = []
    for at in [1, 2, 0, 3]:
        start = at * count
        blocks = march(
            volume,
            coef,
            info,
            row_halo,
            left_halo if at == 0 else None,
            right_halo if at == chunks - 1 else None,
            start,
            count,
            2,
            bumps,
            parts,
        )
        coded = [
            lax.ppermute(blocks[k], "depth", [(i, (i + k) % parts) for i in range(parts)])
            for k in range(1, parts)
        ]
        waiting.append((start, blocks[0], coded))
    for start, own, coded in waiting:
        image = composite(own, coded, info, order, image, start, cols)
    return image[None]


def solution(mesh):
    placed = (
        P("depth", None, "row", "col"),
        P(),
        P("depth", "row", "col"),
        P(),
        P(),
        P(),
        P(),
        P(),
    )
    return jax.shard_map(
        per_device,
        mesh=mesh,
        in_specs=placed,
        out_specs=P("row", None, "depth", "col"),
        check_vma=False,
    )
```

```python
import math

import jax
import jax.numpy as jnp
from jax import lax
from jax.experimental import pallas as pl
from jax.experimental.pallas import tpu as pltpu
from jax.sharding import PartitionSpec as P

absorption = 0.08
LOG2E = math.log2(math.e)
LANES = 128
SUB = 8
GROUP = 2
EDGES_AFTER = False
LAG = 2
STEP = 8
WIDE = 4
UNROLL = 2
LOG_MID = -12.5
LOG_HALF = 16.0
LOG_STEPS = 32767
LOW = -LOG_STEPS
VALUE_FLOOR = 2.0 ** (LOG_MID - LOG_HALF)


def encode(value):
    scale = LOG_STEPS / LOG_HALF
    log2v = jnp.log(jnp.maximum(value, VALUE_FLOOR)) * (scale / math.log(2.0))
    shifted = jnp.clip(log2v + (32768.5 - LOG_MID * scale), 1.0, 65535.5)
    return (shifted.astype(jnp.int32) - 32768).astype(jnp.int16)


def decode(code):
    wide = code.astype(jnp.int32).astype(jnp.float32)
    value = jnp.exp2(wide * (LOG_HALF / LOG_STEPS) + LOG_MID)
    return jnp.where(wide > LOW, value, 0.0)


def march(volume, params, info, row_halo, halos, shift, tile_at, count, tiles, bumps, parts):
    planes, rows, cols = volume.shape
    depth_len = planes - 2
    width = tiles * LANES
    steps = count // tiles
    all_tiles = cols // LANES
    block = rows // parts
    bands = block // SUB
    own = shift == 0
    starts = [(tile_at + i * tiles) % all_tiles for i in range(steps)]
    left_steps = [i for i, t in enumerate(starts) if t == 0]
    right_steps = [i for i, t in enumerate(starts) if t + tiles == all_tiles]
    edges = bool(left_steps or right_steps)
    unroll = min(UNROLL, bands)

    def target(info_ref):
        return lax.rem(info_ref[0] + shift, parts)

    def tile_of(i):
        return lax.rem(tile_at + i * tiles, all_tiles)

    def body(info_ref, param_ref, vol, above, below, left, right, halo, *rest):
        rest = list(rest)
        ends = rest.pop(0) if edges else None
        out, cells, layer, coef = rest
        step = pl.program_id(0)
        row_at, row_last, is_empty = info_ref[1], info_ref[2], info_ref[3]
        to = target(info_ref)

        @pl.when(is_empty == 1)
        def _():
            out[...] = jnp.full(out.shape, 0.0 if own else LOW, out.dtype)

        @pl.when(is_empty != 1)
        def _():
            for t in range(tiles):
                span = slice(LANES * t, LANES * (t + 1))
                cells[t, :, 0:SUB, :] = above[:, :, span].astype(jnp.float32)
                cells[t, :, SUB : SUB + block, :] = vol[:, :, span].astype(jnp.float32)
                cells[t, :, SUB + block :, :] = below[:, :, span].astype(jnp.float32)

            def edge_rows(at, line, switch):
                for t in range(tiles):
                    edge = halo[:, line, LANES * t : LANES * (t + 1)].astype(jnp.float32) * switch
                    cells[t, :, at : at + SUB, :] = jnp.broadcast_to(edge, (planes, SUB, LANES))

            @pl.when(to == 0)
            def _():
                edge_rows(0, slice(0, 1), (row_at > 0).astype(jnp.float32))

            @pl.when(to == parts - 1)
            def _():
                lines = row_halo.shape[1]
                edge_rows(SUB + block, slice(lines - 1, lines), (row_at < row_last).astype(jnp.float32))

            low_half = lax.broadcasted_iota(jnp.int32, (planes, block, LANES), 2) < LANES // 2

            def side(right_tile, left_tile):
                mixed = jnp.where(low_half, right_tile[...], left_tile[...])
                cells[tiles, :, SUB : SUB + block, :] = mixed.astype(jnp.float32)

            side(right, left)
            for at in sorted(set(left_steps + right_steps)):
                pl.when(step == at)(
                    lambda at=at: side(ends if at in right_steps else right, ends if at in left_steps else left)
                )

            def splat(at):
                return jnp.full((SUB, LANES), param_ref[at], jnp.float32)

            square, linear, constant, mix = [], [], [], []
            for k in range(bumps):
                center, spread = splat(k), splat(bumps + k)
                strength = splat(2 * bumps + k) * (absorption / depth_len * LOG2E)
                sq = (-0.5 * LOG2E) / (spread * spread)
                square.append(sq)
                linear.append(-2.0 * sq * center)
                constant.append(sq * center * center + jnp.log(strength) * LOG2E)
                mix.append(1.0 / strength)
            color = [[splat(3 * bumps + c * bumps + k) * mix[k] for k in range(bumps)] for c in range(3)]
            light = [0.7 * splat(6 * bumps + k) for k in range(3)]
            kept = square + linear + constant + light + color[0] + color[1] + color[2]
            for k, value in enumerate(kept):
                coef[k] = value

            lane = lax.broadcasted_iota(jnp.int32, (SUB, LANES), 1)
            first = lane == 0
            last = lane == LANES - 1

            def strip(i, group):
                base = pl.multiple_of(i * SUB, SUB)
                at = list(range(group, min(group + GROUP, tiles)))
                wide = range(len(at))

                def load(t, s, shift=0):
                    return cells[t, s, pl.ds(base + (SUB + shift), SUB), :]

                values = iter([coef[k] for k in range(len(kept))])
                square = [next(values) for k in range(bumps)]
                linear = [next(values) for k in range(bumps)]
                constant = [next(values) for k in range(bumps)]
                light = [next(values) for k in range(3)]
                color = [[next(values) for k in range(bumps)] for c in range(3)]
                zero = jnp.zeros((SUB, LANES), jnp.float32)
                before = [load(t, 0) for t in at]
                here = [load(t, 1) for t in at]
                depth = [zero for t in at]
                through = [zero + 1.0 for t in at]
                total = [[zero] * bumps for t in at]
                for s in range(1, depth_len + 1):
                    ahead = [load(t, s + 1) for t in at]
                    outer_left = load(at[0] - 1 if at[0] > 0 else tiles, s)
                    outer_right = load(at[-1] + 1, s)
                    up = [pltpu.roll(x, 1, 1) for x in [outer_left] + here]
                    down = [pltpu.roll(x, LANES - 1, 1) for x in here + [outer_right]]
                    for j in wide:
                        f = here[j]
                        grad_z = ahead[j] - before[j]
                        grad_y = load(at[j], s, 1) - load(at[j], s, -1)
                        grad_x = jnp.where(last, down[j + 1], down[j]) - jnp.where(first, up[j], up[j + 1])
                        facing = jnp.abs(light[0] * grad_z + light[1] * grad_y + light[2] * grad_x)
                        norm = grad_z * grad_z + grad_y * grad_y + grad_x * grad_x + 4.0
                        shading = 0.3 + facing * lax.rsqrt(norm)
                        bump = [
                            jnp.exp2((square[k] * f + linear[k]) * f + constant[k]) for k in range(bumps)
                        ]
                        density = bump[0]
                        for k in range(1, bumps):
                            density = density + bump[k]
                        depth[j] = depth[j] - density
                        passed = jnp.exp2(depth[j])
                        weight = (through[j] - passed) * shading
                        through[j] = passed
                        total[j] = [total[j][k] + weight * bump[k] for k in range(bumps)]
                    before, here = here, ahead
                for j in wide:
                    span = slice(LANES * at[j], LANES * (at[j] + 1))
                    for c in range(3):
                        mixed = color[c][0] * total[j][0]
                        for k in range(1, bumps):
                            mixed = mixed + color[c][k] * total[j][k]
                        layer[c, pl.ds(base, SUB), span] = mixed
                    layer[3, pl.ds(base, SUB), span] = 1.0 - through[j]

            for group in range(0, tiles, GROUP):

                def some(i, carry, group=group):
                    for part in range(unroll):
                        strip(i * unroll + part, group)
                    return carry

                lax.fori_loop(0, bands // unroll, some, 0)
            out[...] = layer[...] if own else encode(layer[...])

    in_specs = [
        pl.BlockSpec(memory_space=pltpu.SMEM),
        pl.BlockSpec((planes, block, width), lambda i, n: (0, target(n), tile_of(i) // tiles)),
        pl.BlockSpec(
            (planes, SUB, width), lambda i, n: (0, jnp.maximum(target(n) * bands - 1, 0), tile_of(i) // tiles)
        ),
        pl.BlockSpec(
            (planes, SUB, width),
            lambda i, n: (0, jnp.minimum((target(n) + 1) * bands, rows // SUB - 1), tile_of(i) // tiles),
        ),
        pl.BlockSpec((planes, block, LANES), lambda i, n: (0, target(n), jnp.maximum(tile_of(i) - 1, 0))),
        pl.BlockSpec(
            (planes, block, LANES), lambda i, n: (0, target(n), jnp.minimum(tile_of(i) + tiles, all_tiles - 1))
        ),
        pl.BlockSpec((planes, row_halo.shape[1], width), lambda i, n: (0, 0, tile_of(i) // tiles)),
    ]
    operands = [params, volume, volume, volume, volume, volume, row_halo]
    if edges:
        in_specs += [pl.BlockSpec((planes, block, LANES), lambda i, n: (0, target(n), 0))]
        operands.append(halos)
    return pl.pallas_call(
        body,
        out_shape=jax.ShapeDtypeStruct((4, block, count * LANES), jnp.float32 if own else jnp.int16),
        grid_spec=pltpu.PrefetchScalarGridSpec(
            num_scalar_prefetch=1,
            grid=(steps,),
            in_specs=in_specs,
            out_specs=pl.BlockSpec((4, block, width), lambda i, n: (0, 0, i)),
            scratch_shapes=[
                pltpu.VMEM((tiles + 1, planes, block + 2 * SUB, LANES), jnp.float32),
                pltpu.VMEM((4, block, width), jnp.float32),
                pltpu.VMEM((6 * bumps + 3, SUB, LANES), jnp.float32),
            ],
        ),
        compiler_params=pltpu.CompilerParams(vmem_limit_bytes=48 << 20),
        name="march",
    )(info, *operands)


def composite(pieces, info, order, parts, wide):
    channels, block, cols = pieces[0][0][1].shape
    all_tiles = cols // LANES
    steps = all_tiles // wide
    flat = [(k, at, x) for k in range(parts) for at, x in pieces[k]]

    def index_map(at, x):
        held = x.shape[2] // (LANES * wide)

        def index(j, *scalars):
            return (0, 0, jnp.minimum(lax.rem(j + steps - at // wide, steps), held - 1))

        return index

    def body(info_ref, order_ref, *rest):
        out, layers = rest[-2], rest[-1]
        step = pl.program_id(0)
        for (k, at, x), ref in zip(flat, rest):
            held = x.shape[2] // (LANES * wide)

            def fill(k=k, ref=ref):
                layers[k] = ref[...] if k == 0 else decode(ref[...])

            if held == steps:
                fill()
            else:
                pl.when(lax.rem(step + steps - at // wide, steps) < held)(fill)
        me = info_ref[0]

        def band(i, carry):
            row = pl.ds(pl.multiple_of(i * SUB, SUB), SUB)
            through = jnp.ones((SUB, wide * LANES), jnp.float32)
            summed = [jnp.zeros((SUB, wide * LANES), jnp.float32)] * channels
            for place in range(parts):
                at = lax.rem(me - order_ref[place] + parts, parts)
                layer = [layers[at, c, row, :] for c in range(channels)]
                summed = [summed[c] + through * layer[c] for c in range(channels)]
                through = through * (1.0 - layer[3])
            for c in range(channels):
                out[c, row, :] = summed[c]
            return carry

        lax.fori_loop(0, block // SUB, band, 0)

    return pl.pallas_call(
        body,
        grid_spec=pltpu.PrefetchScalarGridSpec(
            num_scalar_prefetch=2,
            grid=(steps,),
            in_specs=[pl.BlockSpec((channels, block, wide * LANES), index_map(at, x)) for k, at, x in flat],
            out_specs=pl.BlockSpec((channels, block, wide * LANES), lambda j, *n: (0, 0, j)),
            scratch_shapes=[pltpu.VMEM((parts, channels, block, wide * LANES), jnp.float32)],
        ),
        out_shape=jax.ShapeDtypeStruct((channels, block, cols), jnp.float32),
        compiler_params=pltpu.CompilerParams(vmem_limit_bytes=48 << 20),
        name="composite",
    )(info, order, *[x for k, at, x in flat])


def plan(parts, all_tiles):
    half, quarter = all_tiles // 2, all_tiles // 4
    far = parts // 2
    pieces = [(k, 0, all_tiles) for k in range(1, parts) if k != far]
    pieces.insert(0, (far, quarter, half))
    pieces.insert(2, (far, quarter + half, half))
    pieces.append((0, 0, all_tiles))
    return [(k, at, count, math.gcd(STEP, quarter if k == far else count)) for k, at, count in pieces]


def per_device(volume, order, empty, bump_center, bump_width, bump_height, bump_color, light_dir):
    volume = volume[0]
    planes, rows, cols = volume.shape
    parts = lax.axis_size("depth")
    n_row = lax.axis_size("row")
    n_col = lax.axis_size("col")
    bumps = bump_center.shape[0]
    row_at = lax.axis_index("row")

    up = [(i, i + 1) for i in range(n_row - 1)]
    down = [(i + 1, i) for i in range(n_row - 1)]
    if n_row == 2:
        edge = lax.dynamic_slice(volume, (0, jnp.where(row_at == 0, rows - 1, 0), 0), (planes, 1, cols))
        row_halo = lax.ppermute(edge, "row", up + down)
    else:
        row_halo = jnp.concatenate(
            [
                lax.ppermute(volume[:, -1:], "row", up),
                lax.ppermute(volume[:, :1], "row", down),
            ],
            axis=1,
        )
    params = jnp.concatenate([bump_center, bump_width, bump_height, bump_color.reshape(-1), light_dir])
    me = lax.axis_index("depth")
    info = jnp.stack([me, row_at, jnp.int32(n_row - 1), empty[0, 0, 0]]).astype(jnp.int32)

    all_tiles = cols // LANES
    pieces = {k: [] for k in range(parts)}
    halos = None
    sent = []
    marched = []
    for turn, (shift, at, count, tiles) in enumerate(plan(parts, all_tiles)):
        if halos is None and (turn == 1 or not EDGES_AFTER):
            ends = (volume[:, :, cols - 1], volume[:, :, 0])
            if EDGES_AFTER:
                *ends, _ = lax.optimization_barrier((*ends, marched[0]))
            before = lax.ppermute(ends[0], "col", [(i, i + 1) for i in range(n_col - 1)])
            after = lax.ppermute(ends[1], "col", [(i + 1, i) for i in range(n_col - 1)])
            low_half = lax.broadcasted_iota(jnp.int32, (planes, rows, LANES), 2) < LANES // 2
            halos = jnp.where(low_half, after[:, :, None], before[:, :, None])
        if turn > 0:
            params, _ = lax.optimization_barrier((params, marched[-1]))
        if turn >= LAG:
            sent[turn - LAG], params = lax.optimization_barrier((sent[turn - LAG], params))
        layer = march(volume, params, info, row_halo, halos, shift, at, count, tiles, bumps, parts)
        marched.append(layer)
        if shift != 0:
            layer = lax.ppermute(layer, "depth", [(i, (i + shift) % parts) for i in range(parts)])
        pieces[shift].append((at, len(sent)))
        sent.append(layer)
    pieces = {k: [(at, sent[n]) for at, n in held] for k, held in pieces.items()}
    return composite(pieces, info, order, parts, math.gcd(WIDE, all_tiles // 4))[None]


def solution(mesh):
    placed = (
        P("depth", None, "row", "col"),
        P(),
        P("depth", "row", "col"),
        P(),
        P(),
        P(),
        P(),
        P(),
    )
    return jax.shard_map(
        per_device,
        mesh=mesh,
        in_specs=placed,
        out_specs=P("row", None, "depth", "col"),
        check_vma=False,
    )
```

```python
import math

import jax
import jax.numpy as jnp
from jax import lax
from jax.experimental import pallas as pl
from jax.experimental.pallas import tpu as pltpu
from jax.sharding import PartitionSpec as P

absorption = 0.08
LOG2E = math.log2(math.e)
LANES = 128
SUB = 8
GROUP = 2
EDGES_AFTER = False
LAG = 9
SPLIT = 1
STEP = 8
WIDE = 4
UNROLL = 2
LOG_MID = -12.5
LOG_HALF = 16.0
LOG_STEPS = 32767
LOW = -LOG_STEPS
VALUE_FLOOR = 2.0 ** (LOG_MID - LOG_HALF)


def encode(value):
    scale = LOG_STEPS / LOG_HALF
    log2v = jnp.log(jnp.maximum(value, VALUE_FLOOR)) * (scale / math.log(2.0))
    shifted = jnp.clip(log2v + (32768.5 - LOG_MID * scale), 1.0, 65535.5)
    return (shifted.astype(jnp.int32) - 32768).astype(jnp.int16)


def decode(code):
    wide = code.astype(jnp.int32).astype(jnp.float32)
    value = jnp.exp2(wide * (LOG_HALF / LOG_STEPS) + LOG_MID)
    return jnp.where(wide > LOW, value, 0.0)


def march(volume, params, info, row_halo, halos, shift, tile_at, count, tiles, bumps, parts):
    planes, rows, cols = volume.shape
    depth_len = planes - 2
    width = tiles * LANES
    steps = count // tiles
    all_tiles = cols // LANES
    block = rows // parts
    bands = block // SUB
    own = shift == 0
    starts = [(tile_at + i * tiles) % all_tiles for i in range(steps)]
    left_steps = [i for i, t in enumerate(starts) if t == 0]
    right_steps = [i for i, t in enumerate(starts) if t + tiles == all_tiles]
    edges = bool(left_steps or right_steps)
    unroll = min(UNROLL, bands)

    def target(info_ref):
        return lax.rem(info_ref[0] + shift, parts)

    def tile_of(i):
        return lax.rem(tile_at + i * tiles, all_tiles)

    def body(info_ref, param_ref, vol, above, below, left, right, halo, *rest):
        rest = list(rest)
        ends = rest.pop(0) if edges else None
        out, cells, layer, coef = rest
        step = pl.program_id(0)
        row_at, row_last, is_empty = info_ref[1], info_ref[2], info_ref[3]
        to = target(info_ref)

        @pl.when(is_empty == 1)
        def _():
            out[...] = jnp.full(out.shape, 0.0 if own else LOW, out.dtype)

        @pl.when(is_empty != 1)
        def _():
            for t in range(tiles):
                span = slice(LANES * t, LANES * (t + 1))
                cells[t, :, 0:SUB, :] = above[:, :, span].astype(jnp.float32)
                cells[t, :, SUB : SUB + block, :] = vol[:, :, span].astype(jnp.float32)
                cells[t, :, SUB + block :, :] = below[:, :, span].astype(jnp.float32)

            def edge_rows(at, line, switch):
                for t in range(tiles):
                    edge = halo[:, line, LANES * t : LANES * (t + 1)].astype(jnp.float32) * switch
                    cells[t, :, at : at + SUB, :] = jnp.broadcast_to(edge, (planes, SUB, LANES))

            @pl.when(to == 0)
            def _():
                edge_rows(0, slice(0, 1), (row_at > 0).astype(jnp.float32))

            @pl.when(to == parts - 1)
            def _():
                lines = row_halo.shape[1]
                edge_rows(SUB + block, slice(lines - 1, lines), (row_at < row_last).astype(jnp.float32))

            low_half = lax.broadcasted_iota(jnp.int32, (planes, block, LANES), 2) < LANES // 2

            def side(right_tile, left_tile):
                mixed = jnp.where(low_half, right_tile[...], left_tile[...])
                cells[tiles, :, SUB : SUB + block, :] = mixed.astype(jnp.float32)

            side(right, left)
            for at in sorted(set(left_steps + right_steps)):
                pl.when(step == at)(
                    lambda at=at: side(ends if at in right_steps else right, ends if at in left_steps else left)
                )

            def splat(at):
                return jnp.full((SUB, LANES), param_ref[at], jnp.float32)

            square, linear, constant, mix = [], [], [], []
            for k in range(bumps):
                center, spread = splat(k), splat(bumps + k)
                strength = splat(2 * bumps + k) * (absorption / depth_len * LOG2E)
                sq = (-0.5 * LOG2E) / (spread * spread)
                square.append(sq)
                linear.append(-2.0 * sq * center)
                constant.append(sq * center * center + jnp.log(strength) * LOG2E)
                mix.append(1.0 / strength)
            color = [[splat(3 * bumps + c * bumps + k) * mix[k] for k in range(bumps)] for c in range(3)]
            light = [0.7 * splat(6 * bumps + k) for k in range(3)]
            kept = square + linear + constant + light + color[0] + color[1] + color[2]
            for k, value in enumerate(kept):
                coef[k] = value

            lane = lax.broadcasted_iota(jnp.int32, (SUB, LANES), 1)
            first = lane == 0
            last = lane == LANES - 1

            def strip(i, group):
                base = pl.multiple_of(i * SUB, SUB)
                at = list(range(group, min(group + GROUP, tiles)))
                wide = range(len(at))

                def load(t, s, shift=0):
                    return cells[t, s, pl.ds(base + (SUB + shift), SUB), :]

                values = iter([coef[k] for k in range(len(kept))])
                square = [next(values) for k in range(bumps)]
                linear = [next(values) for k in range(bumps)]
                constant = [next(values) for k in range(bumps)]
                light = [next(values) for k in range(3)]
                color = [[next(values) for k in range(bumps)] for c in range(3)]
                zero = jnp.zeros((SUB, LANES), jnp.float32)
                before = [load(t, 0) for t in at]
                here = [load(t, 1) for t in at]
                depth = [zero for t in at]
                through = [zero + 1.0 for t in at]
                total = [[zero] * bumps for t in at]
                for s in range(1, depth_len + 1):
                    ahead = [load(t, s + 1) for t in at]
                    outer_left = load(at[0] - 1 if at[0] > 0 else tiles, s)
                    outer_right = load(at[-1] + 1, s)
                    up = [pltpu.roll(x, 1, 1) for x in [outer_left] + here]
                    down = [pltpu.roll(x, LANES - 1, 1) for x in here + [outer_right]]
                    for j in wide:
                        f = here[j]
                        grad_z = ahead[j] - before[j]
                        grad_y = load(at[j], s, 1) - load(at[j], s, -1)
                        grad_x = jnp.where(last, down[j + 1], down[j]) - jnp.where(first, up[j], up[j + 1])
                        facing = jnp.abs(light[0] * grad_z + light[1] * grad_y + light[2] * grad_x)
                        norm = grad_z * grad_z + grad_y * grad_y + grad_x * grad_x + 4.0
                        shading = 0.3 + facing * lax.rsqrt(norm)
                        bump = [
                            jnp.exp2((square[k] * f + linear[k]) * f + constant[k]) for k in range(bumps)
                        ]
                        density = bump[0]
                        for k in range(1, bumps):
                            density = density + bump[k]
                        depth[j] = depth[j] - density
                        passed = jnp.exp2(depth[j])
                        weight = (through[j] - passed) * shading
                        through[j] = passed
                        total[j] = [total[j][k] + weight * bump[k] for k in range(bumps)]
                    before, here = here, ahead
                for j in wide:
                    span = slice(LANES * at[j], LANES * (at[j] + 1))
                    for c in range(3):
                        mixed = color[c][0] * total[j][0]
                        for k in range(1, bumps):
                            mixed = mixed + color[c][k] * total[j][k]
                        layer[c, pl.ds(base, SUB), span] = mixed
                    layer[3, pl.ds(base, SUB), span] = 1.0 - through[j]

            for group in range(0, tiles, GROUP):

                def some(i, carry, group=group):
                    for part in range(unroll):
                        strip(i * unroll + part, group)
                    return carry

                lax.fori_loop(0, bands // unroll, some, 0)
            out[...] = layer[...] if own else encode(layer[...])

    in_specs = [
        pl.BlockSpec(memory_space=pltpu.SMEM),
        pl.BlockSpec((planes, block, width), lambda i, n: (0, target(n), tile_of(i) // tiles)),
        pl.BlockSpec(
            (planes, SUB, width), lambda i, n: (0, jnp.maximum(target(n) * bands - 1, 0), tile_of(i) // tiles)
        ),
        pl.BlockSpec(
            (planes, SUB, width),
            lambda i, n: (0, jnp.minimum((target(n) + 1) * bands, rows // SUB - 1), tile_of(i) // tiles),
        ),
        pl.BlockSpec((planes, block, LANES), lambda i, n: (0, target(n), jnp.maximum(tile_of(i) - 1, 0))),
        pl.BlockSpec(
            (planes, block, LANES), lambda i, n: (0, target(n), jnp.minimum(tile_of(i) + tiles, all_tiles - 1))
        ),
        pl.BlockSpec((planes, row_halo.shape[1], width), lambda i, n: (0, 0, tile_of(i) // tiles)),
    ]
    operands = [params, volume, volume, volume, volume, volume, row_halo]
    if edges:
        in_specs += [pl.BlockSpec((planes, block, LANES), lambda i, n: (0, target(n), 0))]
        operands.append(halos)
    return pl.pallas_call(
        body,
        out_shape=jax.ShapeDtypeStruct((4, block, count * LANES), jnp.float32 if own else jnp.int16),
        grid_spec=pltpu.PrefetchScalarGridSpec(
            num_scalar_prefetch=1,
            grid=(steps,),
            in_specs=in_specs,
            out_specs=pl.BlockSpec((4, block, width), lambda i, n: (0, 0, i)),
            scratch_shapes=[
                pltpu.VMEM((tiles + 1, planes, block + 2 * SUB, LANES), jnp.float32),
                pltpu.VMEM((4, block, width), jnp.float32),
                pltpu.VMEM((6 * bumps + 3, SUB, LANES), jnp.float32),
            ],
        ),
        compiler_params=pltpu.CompilerParams(vmem_limit_bytes=48 << 20),
        name="march",
    )(info, *operands)


def composite(pieces, info, order, parts, wide):
    channels, block, cols = pieces[0][0][1].shape
    all_tiles = cols // LANES
    steps = all_tiles // wide
    flat = [(k, at, x) for k in range(parts) for at, x in pieces[k]]

    def index_map(at, x):
        held = x.shape[2] // (LANES * wide)

        def index(j, *scalars):
            return (0, 0, jnp.minimum(lax.rem(j + steps - at // wide, steps), held - 1))

        return index

    def body(info_ref, order_ref, *rest):
        out, layers = rest[-2], rest[-1]
        step = pl.program_id(0)
        for (k, at, x), ref in zip(flat, rest):
            held = x.shape[2] // (LANES * wide)

            def fill(k=k, ref=ref):
                layers[k] = ref[...] if k == 0 else decode(ref[...])

            if held == steps:
                fill()
            else:
                pl.when(lax.rem(step + steps - at // wide, steps) < held)(fill)
        me = info_ref[0]

        def band(i, carry):
            row = pl.ds(pl.multiple_of(i * SUB, SUB), SUB)
            through = jnp.ones((SUB, wide * LANES), jnp.float32)
            summed = [jnp.zeros((SUB, wide * LANES), jnp.float32)] * channels
            for place in range(parts):
                at = lax.rem(me - order_ref[place] + parts, parts)
                layer = [layers[at, c, row, :] for c in range(channels)]
                summed = [summed[c] + through * layer[c] for c in range(channels)]
                through = through * (1.0 - layer[3])
            for c in range(channels):
                out[c, row, :] = summed[c]
            return carry

        lax.fori_loop(0, block // SUB, band, 0)

    return pl.pallas_call(
        body,
        grid_spec=pltpu.PrefetchScalarGridSpec(
            num_scalar_prefetch=2,
            grid=(steps,),
            in_specs=[pl.BlockSpec((channels, block, wide * LANES), index_map(at, x)) for k, at, x in flat],
            out_specs=pl.BlockSpec((channels, block, wide * LANES), lambda j, *n: (0, 0, j)),
            scratch_shapes=[pltpu.VMEM((parts, channels, block, wide * LANES), jnp.float32)],
        ),
        out_shape=jax.ShapeDtypeStruct((channels, block, cols), jnp.float32),
        compiler_params=pltpu.CompilerParams(vmem_limit_bytes=48 << 20),
        name="composite",
    )(info, order, *[x for k, at, x in flat])


def plan(parts, all_tiles):
    far = parts // 2
    shifts = [far] + [k for k in range(1, parts) if k != far]
    half, quarter = all_tiles // 2, all_tiles // 4
    pieces = []
    for turn, k in enumerate(shifts + [0]):
        if turn < SPLIT and k != 0:
            pieces.append((turn, k, quarter, half))
            pieces.append((turn + SPLIT, k, quarter + half, half))
        else:
            pieces.append((turn + 2 * SPLIT, k, 0, all_tiles))
    return [(k, at, count, math.gcd(STEP, quarter if count == half else count)) for turn, k, at, count in sorted(pieces)]


def per_device(volume, order, empty, bump_center, bump_width, bump_height, bump_color, light_dir):
    volume = volume[0]
    planes, rows, cols = volume.shape
    parts = lax.axis_size("depth")
    n_row = lax.axis_size("row")
    n_col = lax.axis_size("col")
    bumps = bump_center.shape[0]
    row_at = lax.axis_index("row")

    up = [(i, i + 1) for i in range(n_row - 1)]
    down = [(i + 1, i) for i in range(n_row - 1)]
    if n_row == 2:
        edge = lax.dynamic_slice(volume, (0, jnp.where(row_at == 0, rows - 1, 0), 0), (planes, 1, cols))
        row_halo = lax.ppermute(edge, "row", up + down)
    else:
        row_halo = jnp.concatenate(
            [
                lax.ppermute(volume[:, -1:], "row", up),
                lax.ppermute(volume[:, :1], "row", down),
            ],
            axis=1,
        )
    params = jnp.concatenate([bump_center, bump_width, bump_height, bump_color.reshape(-1), light_dir])
    me = lax.axis_index("depth")
    info = jnp.stack([me, row_at, jnp.int32(n_row - 1), empty[0, 0, 0]]).astype(jnp.int32)

    all_tiles = cols // LANES
    pieces = {k: [] for k in range(parts)}
    halos = None
    sent = []
    marched = []
    for turn, (shift, at, count, tiles) in enumerate(plan(parts, all_tiles)):
        if halos is None and (turn == 1 or not EDGES_AFTER):
            ends = (volume[:, :, cols - 1], volume[:, :, 0])
            if EDGES_AFTER:
                *ends, _ = lax.optimization_barrier((*ends, marched[0]))
            before = lax.ppermute(ends[0], "col", [(i, i + 1) for i in range(n_col - 1)])
            after = lax.ppermute(ends[1], "col", [(i + 1, i) for i in range(n_col - 1)])
            low_half = lax.broadcasted_iota(jnp.int32, (planes, rows, LANES), 2) < LANES // 2
            halos = jnp.where(low_half, after[:, :, None], before[:, :, None])
        if turn > 0:
            params, _ = lax.optimization_barrier((params, marched[-1]))
        if turn >= LAG:
            sent[turn - LAG], params = lax.optimization_barrier((sent[turn - LAG], params))
        layer = march(volume, params, info, row_halo, halos, shift, at, count, tiles, bumps, parts)
        marched.append(layer)
        if shift != 0:
            if turn >= 2:
                sent[turn - 2], layer = lax.optimization_barrier((sent[turn - 2], layer))
            layer = lax.ppermute(layer, "depth", [(i, (i + shift) % parts) for i in range(parts)])
        pieces[shift].append((at, len(sent)))
        sent.append(layer)
    pieces = {k: [(at, sent[n]) for at, n in held] for k, held in pieces.items()}
    return composite(pieces, info, order, parts, math.gcd(WIDE, all_tiles // 4))[None]


def solution(mesh):
    placed = (
        P("depth", None, "row", "col"),
        P(),
        P("depth", "row", "col"),
        P(),
        P(),
        P(),
        P(),
        P(),
    )
    return jax.shard_map(
        per_device,
        mesh=mesh,
        in_specs=placed,
        out_specs=P("row", None, "depth", "col"),
        check_vma=False,
    )
```

```python
import math

import jax
import jax.numpy as jnp
from jax import lax
from jax.experimental import pallas as pl
from jax.experimental.pallas import tpu as pltpu
from jax.sharding import PartitionSpec as P

absorption = 0.08
LOG2E = math.log2(math.e)
LANES = 128
SUB = 8
GROUP = 2
EDGES_AFTER = False
LAG = 3
SPLIT = 1
STEP = 8
WIDE = 4
UNROLL = 2
LOG_MID = -12.5
LOG_HALF = 16.0
LOG_STEPS = 32767
LOW = -LOG_STEPS
VALUE_FLOOR = 2.0 ** (LOG_MID - LOG_HALF)


def encode(value):
    scale = LOG_STEPS / LOG_HALF
    log2v = jnp.log(jnp.maximum(value, VALUE_FLOOR)) * (scale / math.log(2.0))
    shifted = jnp.clip(log2v + (32768.5 - LOG_MID * scale), 1.0, 65535.5)
    return (shifted.astype(jnp.int32) - 32768).astype(jnp.int16)


def decode(code):
    wide = code.astype(jnp.int32).astype(jnp.float32)
    value = jnp.exp2(wide * (LOG_HALF / LOG_STEPS) + LOG_MID)
    return jnp.where(wide > LOW, value, 0.0)


def march(volume, params, info, row_halo, halos, shift, tile_at, count, tiles, bumps, parts):
    planes, rows, cols = volume.shape
    depth_len = planes - 2
    width = tiles * LANES
    steps = count // tiles
    all_tiles = cols // LANES
    block = rows // parts
    bands = block // SUB
    own = shift == 0
    starts = [(tile_at + i * tiles) % all_tiles for i in range(steps)]
    left_steps = [i for i, t in enumerate(starts) if t == 0]
    right_steps = [i for i, t in enumerate(starts) if t + tiles == all_tiles]
    edges = bool(left_steps or right_steps)
    unroll = min(UNROLL, bands)

    def target(info_ref):
        return lax.rem(info_ref[0] + shift, parts)

    def tile_of(i):
        return lax.rem(tile_at + i * tiles, all_tiles)

    def body(info_ref, param_ref, vol, above, below, left, right, halo, *rest):
        rest = list(rest)
        ends = rest.pop(0) if edges else None
        out, cells, layer, coef = rest
        step = pl.program_id(0)
        row_at, row_last, is_empty = info_ref[1], info_ref[2], info_ref[3]
        to = target(info_ref)

        @pl.when(is_empty == 1)
        def _():
            out[...] = jnp.full(out.shape, 0.0 if own else LOW, out.dtype)

        @pl.when(is_empty != 1)
        def _():
            for t in range(tiles):
                span = slice(LANES * t, LANES * (t + 1))
                cells[t, :, 0:SUB, :] = above[:, :, span].astype(jnp.float32)
                cells[t, :, SUB : SUB + block, :] = vol[:, :, span].astype(jnp.float32)
                cells[t, :, SUB + block :, :] = below[:, :, span].astype(jnp.float32)

            def edge_rows(at, line, switch):
                for t in range(tiles):
                    edge = halo[:, line, LANES * t : LANES * (t + 1)].astype(jnp.float32) * switch
                    cells[t, :, at : at + SUB, :] = jnp.broadcast_to(edge, (planes, SUB, LANES))

            @pl.when(to == 0)
            def _():
                edge_rows(0, slice(0, 1), (row_at > 0).astype(jnp.float32))

            @pl.when(to == parts - 1)
            def _():
                lines = row_halo.shape[1]
                edge_rows(SUB + block, slice(lines - 1, lines), (row_at < row_last).astype(jnp.float32))

            low_half = lax.broadcasted_iota(jnp.int32, (planes, block, LANES), 2) < LANES // 2

            def side(right_tile, left_tile):
                mixed = jnp.where(low_half, right_tile[...], left_tile[...])
                cells[tiles, :, SUB : SUB + block, :] = mixed.astype(jnp.float32)

            side(right, left)
            for at in sorted(set(left_steps + right_steps)):
                pl.when(step == at)(
                    lambda at=at: side(ends if at in right_steps else right, ends if at in left_steps else left)
                )

            def splat(at):
                return jnp.full((SUB, LANES), param_ref[at], jnp.float32)

            square, linear, constant, mix = [], [], [], []
            for k in range(bumps):
                center, spread = splat(k), splat(bumps + k)
                strength = splat(2 * bumps + k) * (absorption / depth_len * LOG2E)
                sq = (-0.5 * LOG2E) / (spread * spread)
                square.append(sq)
                linear.append(-2.0 * sq * center)
                constant.append(sq * center * center + jnp.log(strength) * LOG2E)
                mix.append(1.0 / strength)
            color = [[splat(3 * bumps + c * bumps + k) * mix[k] for k in range(bumps)] for c in range(3)]
            light = [0.7 * splat(6 * bumps + k) for k in range(3)]
            kept = square + linear + constant + light + color[0] + color[1] + color[2]
            for k, value in enumerate(kept):
                coef[k] = value

            lane = lax.broadcasted_iota(jnp.int32, (SUB, LANES), 1)
            first = lane == 0
            last = lane == LANES - 1

            def strip(i, group):
                base = pl.multiple_of(i * SUB, SUB)
                at = list(range(group, min(group + GROUP, tiles)))
                wide = range(len(at))

                def load(t, s, shift=0):
                    return cells[t, s, pl.ds(base + (SUB + shift), SUB), :]

                values = iter([coef[k] for k in range(len(kept))])
                square = [next(values) for k in range(bumps)]
                linear = [next(values) for k in range(bumps)]
                constant = [next(values) for k in range(bumps)]
                light = [next(values) for k in range(3)]
                color = [[next(values) for k in range(bumps)] for c in range(3)]
                zero = jnp.zeros((SUB, LANES), jnp.float32)
                before = [load(t, 0) for t in at]
                here = [load(t, 1) for t in at]
                depth = [zero for t in at]
                through = [zero + 1.0 for t in at]
                total = [[zero] * bumps for t in at]
                for s in range(1, depth_len + 1):
                    ahead = [load(t, s + 1) for t in at]
                    outer_left = load(at[0] - 1 if at[0] > 0 else tiles, s)
                    outer_right = load(at[-1] + 1, s)
                    up = [pltpu.roll(x, 1, 1) for x in [outer_left] + here]
                    down = [pltpu.roll(x, LANES - 1, 1) for x in here + [outer_right]]
                    for j in wide:
                        f = here[j]
                        grad_z = ahead[j] - before[j]
                        grad_y = load(at[j], s, 1) - load(at[j], s, -1)
                        grad_x = jnp.where(last, down[j + 1], down[j]) - jnp.where(first, up[j], up[j + 1])
                        facing = jnp.abs(light[0] * grad_z + light[1] * grad_y + light[2] * grad_x)
                        norm = grad_z * grad_z + grad_y * grad_y + grad_x * grad_x + 4.0
                        shading = 0.3 + facing * lax.rsqrt(norm)
                        bump = [
                            jnp.exp2((square[k] * f + linear[k]) * f + constant[k]) for k in range(bumps)
                        ]
                        density = bump[0]
                        for k in range(1, bumps):
                            density = density + bump[k]
                        depth[j] = depth[j] - density
                        passed = jnp.exp2(depth[j])
                        weight = (through[j] - passed) * shading
                        through[j] = passed
                        total[j] = [total[j][k] + weight * bump[k] for k in range(bumps)]
                    before, here = here, ahead
                for j in wide:
                    span = slice(LANES * at[j], LANES * (at[j] + 1))
                    for c in range(3):
                        mixed = color[c][0] * total[j][0]
                        for k in range(1, bumps):
                            mixed = mixed + color[c][k] * total[j][k]
                        layer[c, pl.ds(base, SUB), span] = mixed
                    layer[3, pl.ds(base, SUB), span] = 1.0 - through[j]

            for group in range(0, tiles, GROUP):

                def some(i, carry, group=group):
                    for part in range(unroll):
                        strip(i * unroll + part, group)
                    return carry

                lax.fori_loop(0, bands // unroll, some, 0)
            out[...] = layer[...] if own else encode(layer[...])

    in_specs = [
        pl.BlockSpec(memory_space=pltpu.SMEM),
        pl.BlockSpec((planes, block, width), lambda i, n: (0, target(n), tile_of(i) // tiles)),
        pl.BlockSpec(
            (planes, SUB, width), lambda i, n: (0, jnp.maximum(target(n) * bands - 1, 0), tile_of(i) // tiles)
        ),
        pl.BlockSpec(
            (planes, SUB, width),
            lambda i, n: (0, jnp.minimum((target(n) + 1) * bands, rows // SUB - 1), tile_of(i) // tiles),
        ),
        pl.BlockSpec((planes, block, LANES), lambda i, n: (0, target(n), jnp.maximum(tile_of(i) - 1, 0))),
        pl.BlockSpec(
            (planes, block, LANES), lambda i, n: (0, target(n), jnp.minimum(tile_of(i) + tiles, all_tiles - 1))
        ),
        pl.BlockSpec((planes, row_halo.shape[1], width), lambda i, n: (0, 0, tile_of(i) // tiles)),
    ]
    operands = [params, volume, volume, volume, volume, volume, row_halo]
    if edges:
        in_specs += [pl.BlockSpec((planes, block, LANES), lambda i, n: (0, target(n), 0))]
        operands.append(halos)
    return pl.pallas_call(
        body,
        out_shape=jax.ShapeDtypeStruct((4, block, count * LANES), jnp.float32 if own else jnp.int16),
        grid_spec=pltpu.PrefetchScalarGridSpec(
            num_scalar_prefetch=1,
            grid=(steps,),
            in_specs=in_specs,
            out_specs=pl.BlockSpec((4, block, width), lambda i, n: (0, 0, i)),
            scratch_shapes=[
                pltpu.VMEM((tiles + 1, planes, block + 2 * SUB, LANES), jnp.float32),
                pltpu.VMEM((4, block, width), jnp.float32),
                pltpu.VMEM((6 * bumps + 3, SUB, LANES), jnp.float32),
            ],
        ),
        compiler_params=pltpu.CompilerParams(vmem_limit_bytes=48 << 20),
        name="march",
    )(info, *operands)


def composite(pieces, info, order, parts, wide):
    channels, block, cols = pieces[0][0][1].shape
    all_tiles = cols // LANES
    steps = all_tiles // wide
    flat = [(k, at, x) for k in range(parts) for at, x in pieces[k]]

    def index_map(at, x):
        held = x.shape[2] // (LANES * wide)

        def index(j, *scalars):
            return (0, 0, jnp.minimum(lax.rem(j + steps - at // wide, steps), held - 1))

        return index

    def body(info_ref, order_ref, *rest):
        out, layers = rest[-2], rest[-1]
        step = pl.program_id(0)
        for (k, at, x), ref in zip(flat, rest):
            held = x.shape[2] // (LANES * wide)

            def fill(k=k, ref=ref):
                layers[k] = ref[...] if k == 0 else decode(ref[...])

            if held == steps:
                fill()
            else:
                pl.when(lax.rem(step + steps - at // wide, steps) < held)(fill)
        me = info_ref[0]

        def band(i, carry):
            row = pl.ds(pl.multiple_of(i * SUB, SUB), SUB)
            through = jnp.ones((SUB, wide * LANES), jnp.float32)
            summed = [jnp.zeros((SUB, wide * LANES), jnp.float32)] * channels
            for place in range(parts):
                at = lax.rem(me - order_ref[place] + parts, parts)
                layer = [layers[at, c, row, :] for c in range(channels)]
                summed = [summed[c] + through * layer[c] for c in range(channels)]
                through = through * (1.0 - layer[3])
            for c in range(channels):
                out[c, row, :] = summed[c]
            return carry

        lax.fori_loop(0, block // SUB, band, 0)

    return pl.pallas_call(
        body,
        grid_spec=pltpu.PrefetchScalarGridSpec(
            num_scalar_prefetch=2,
            grid=(steps,),
            in_specs=[pl.BlockSpec((channels, block, wide * LANES), index_map(at, x)) for k, at, x in flat],
            out_specs=pl.BlockSpec((channels, block, wide * LANES), lambda j, *n: (0, 0, j)),
            scratch_shapes=[pltpu.VMEM((parts, channels, block, wide * LANES), jnp.float32)],
        ),
        out_shape=jax.ShapeDtypeStruct((channels, block, cols), jnp.float32),
        compiler_params=pltpu.CompilerParams(vmem_limit_bytes=48 << 20),
        name="composite",
    )(info, order, *[x for k, at, x in flat])


def plan(parts, all_tiles):
    far = parts // 2
    shifts = [far] + [k for k in range(1, parts) if k != far]
    half, quarter = all_tiles // 2, all_tiles // 4
    pieces = []
    for turn, k in enumerate(shifts + [0]):
        if turn < SPLIT and k != 0:
            pieces.append((turn, k, quarter, half))
            pieces.append((turn + SPLIT, k, quarter + half, half))
        else:
            pieces.append((turn + 2 * SPLIT, k, 0, all_tiles))
    return [(k, at, count, math.gcd(STEP, quarter if count == half else count)) for turn, k, at, count in sorted(pieces)]


def per_device(volume, order, empty, bump_center, bump_width, bump_height, bump_color, light_dir):
    volume = volume[0]
    planes, rows, cols = volume.shape
    parts = lax.axis_size("depth")
    n_row = lax.axis_size("row")
    n_col = lax.axis_size("col")
    bumps = bump_center.shape[0]
    row_at = lax.axis_index("row")

    up = [(i, i + 1) for i in range(n_row - 1)]
    down = [(i + 1, i) for i in range(n_row - 1)]
    if n_row == 2:
        edge = lax.dynamic_slice(volume, (0, jnp.where(row_at == 0, rows - 1, 0), 0), (planes, 1, cols))
        row_halo = lax.ppermute(edge, "row", up + down)
    else:
        row_halo = jnp.concatenate(
            [
                lax.ppermute(volume[:, -1:], "row", up),
                lax.ppermute(volume[:, :1], "row", down),
            ],
            axis=1,
        )
    params = jnp.concatenate([bump_center, bump_width, bump_height, bump_color.reshape(-1), light_dir])
    me = lax.axis_index("depth")
    info = jnp.stack([me, row_at, jnp.int32(n_row - 1), empty[0, 0, 0]]).astype(jnp.int32)

    all_tiles = cols // LANES
    pieces = {k: [] for k in range(parts)}
    halos = None
    sent = []
    marched = []
    for turn, (shift, at, count, tiles) in enumerate(plan(parts, all_tiles)):
        if halos is None and (turn == 1 or not EDGES_AFTER):
            ends = (volume[:, :, cols - 1], volume[:, :, 0])
            if EDGES_AFTER:
                *ends, _ = lax.optimization_barrier((*ends, marched[0]))
            before = lax.ppermute(ends[0], "col", [(i, i + 1) for i in range(n_col - 1)])
            after = lax.ppermute(ends[1], "col", [(i + 1, i) for i in range(n_col - 1)])
            low_half = lax.broadcasted_iota(jnp.int32, (planes, rows, LANES), 2) < LANES // 2
            halos = jnp.where(low_half, after[:, :, None], before[:, :, None])
        if turn > 0:
            params, _ = lax.optimization_barrier((params, marched[-1]))
        if turn == LAG:
            sent[turn - LAG], params = lax.optimization_barrier((sent[turn - LAG], params))
        layer = march(volume, params, info, row_halo, halos, shift, at, count, tiles, bumps, parts)
        marched.append(layer)
        if shift != 0:
            if turn == 3:
                sent[turn - 2], layer = lax.optimization_barrier((sent[turn - 2], layer))
            layer = lax.ppermute(layer, "depth", [(i, (i + shift) % parts) for i in range(parts)])
        pieces[shift].append((at, len(sent)))
        sent.append(layer)
    pieces = {k: [(at, sent[n]) for at, n in held] for k, held in pieces.items()}
    return composite(pieces, info, order, parts, math.gcd(WIDE, all_tiles // 4))[None]


def solution(mesh):
    placed = (
        P("depth", None, "row", "col"),
        P(),
        P("depth", "row", "col"),
        P(),
        P(),
        P(),
        P(),
        P(),
    )
    return jax.shard_map(
        per_device,
        mesh=mesh,
        in_specs=placed,
        out_specs=P("row", None, "depth", "col"),
        check_vma=False,
    )
```
